32 devices in a mesh: wide: 16 (over z, y, x), cols: 2 (over core).
Axes of the slice: x: 2, y: 2, z: 4, core: 2. Of those that a mesh axis runs over, the one named last changes fastest.
Arguments:
- factor: float32 [32768, 256], P('wide', 'cols')
- gates: float32 [8, 128, 128], replicated, may hold values from -0.5 to 0.5
- gate_layout: int32 [256], P('wide'), may hold values from 0 to 7
- jump_masks: int32 [3], replicated, may hold values from 1 to 15
- jump_rates: float32 [3], replicated, may hold values from 0.1 to 0.4
- sketch_perm: int32 [1024], replicated, may hold values from 0 to 1023, each once
- bases: float32 [8, 64, 64], replicated, may hold values from -0.75 to 0.75
- basis_index: int32 [16, 32], P('wide'), may hold values from 0 to 7
Outputs:
- new_factor: float32 [32768, 256], P('wide', 'cols')
- weights: float32 [16, 2048], P('wide', 'cols')
The draws below stay inside these ranges and needn't reach their ends.
Inputs may be any that keep to these rules, and one draw needn't show every extreme that they name: `jump_masks`: nonzero bit masks over the high qubits. `sketch_perm`: each value appears once.
All inputs are finite; a program needn't handle non-finite values.
Results may differ from the reference program's by a relative error of at most 0.0003.
Values sent between devices are 32-bit elements; how exact they have to be, the bound alone decides.
A program may use at most 64 MiB of HBM per device.

```python
import math
import jax
import jax.numpy as jnp
from jax import lax

ROWS_DEV = 2048
GATE_ORD = 128
ROT_ORD = 64
GATES = 8
BASES = 8
JUMPS = 3
NS_ITERS = 7
ROWS = 32768
RANK = 256
STACK = 1024
N_WIDE = 16


def draw_factor(key, part):
    first, second, third = jax.random.split(jax.random.fold_in(key, 11), 3)
    rough = jnp.exp(jax.random.uniform(second, (ROWS, 1), jnp.float32) * jnp.log(10.0))
    colscale = jnp.exp(jax.random.uniform(third, (1, RANK), jnp.float32) * jnp.log(4.0))
    position = jnp.arange(ROWS, dtype=jnp.float32)[:, None] / ROWS
    base = jax.random.normal(first, (ROWS, RANK), jnp.float32)
    trend = jnp.exp(jnp.log(3.0) * position)
    return (base * rough * trend * colscale / 8.0).astype(jnp.float32)


def set_ends(result, own_key, least, largest):
    shape = result.shape
    place = [jax.random.randint(jax.random.fold_in(own_key, axis), (), 0, shape[axis]) for axis in range(len(shape))]
    result = result.at[tuple(place)].set(least)
    longest = shape.index(max(shape))
    place[longest] = (place[longest] + 1) % shape[longest]
    return result.at[tuple(place)].set(largest)


def scatter_about(stream_key, dims, deviation, bound, kind=jnp.bfloat16):
    return jnp.clip(deviation * jax.random.normal(stream_key, dims, jnp.float32), -bound, bound).astype(kind)


def setup_inputs(seed: int = 0) -> dict:
    seeds = jax.random.split(jax.random.key(seed), 9)
    return {
        "factor": draw_factor(jax.random.fold_in(seeds[8], 71), 0),
        "gates": scatter_about(seeds[1], (GATES, GATE_ORD, GATE_ORD), GATE_ORD ** -0.5, 0.5, jnp.float32),
        "gate_layout": set_ends(jax.random.randint(seeds[2], (ROWS // GATE_ORD,), 0, GATES), jax.random.fold_in(seeds[2], 1), 0, GATES - 1).astype(jnp.int32),
        "jump_masks": jax.random.randint(seeds[3], (JUMPS,), 1, N_WIDE).astype(jnp.int32),
        "jump_rates": jnp.clip(jnp.exp(jax.random.uniform(seeds[4], (JUMPS,), jnp.float32, math.log(0.1), math.log(0.4))), 0.1, 0.4),
        "sketch_perm": jax.random.permutation(seeds[5], STACK).astype(jnp.int32),
        "bases": scatter_about(seeds[6], (BASES, ROT_ORD, ROT_ORD), ROT_ORD ** -0.5, 0.75, jnp.float32),
        "basis_index": set_ends(jax.random.randint(seeds[7], (N_WIDE, ROWS_DEV // ROT_ORD), 0, BASES), jax.random.fold_in(seeds[7], 1), 0, BASES - 1).astype(jnp.int32),
    }


HIGH = lax.Precision.HIGHEST

def apply_blocks(mats, index, data):
    chosen = jnp.take(mats, index, axis=0)
    return jnp.einsum('bij,bjc->bic', chosen, data, precision=HIGH)

def flip_rows(data, mask, count):
    shaped = data.reshape(count, data.shape[0] // count, data.shape[1])
    source = jnp.bitwise_xor(jnp.arange(count, dtype=jnp.int32), mask)
    return jnp.take(shaped, source, axis=0).reshape(data.shape)

def sketch_table(sketch_perm, rank):
    target = sketch_perm % rank
    sign = 1.0 - 2.0 * (sketch_perm // rank % 2).astype(jnp.float32)
    hit = target[:, None] == jnp.arange(rank, dtype=jnp.int32)[None, :]
    return jnp.where(hit, sign[:, None], jnp.zeros((), jnp.float32))

def mixed_stack(source, table, coefs, masks, count):
    rank = table.shape[1]
    total = jnp.zeros((source.shape[0], rank), jnp.float32)
    for k in range(len(coefs)):
        block = table[k * rank:(k + 1) * rank]
        term = coefs[k] * jnp.dot(source, block, precision=HIGH, preferred_element_type=jnp.float32)
        if k > 0:
            term = flip_rows(term, masks[k - 1], count)
        total = total + term
    return total

def project_block(sketch_block, moved_block, coefs, masks, count):
    parts = []
    for k in range(len(coefs)):
        left = sketch_block if k == 0 else flip_rows(sketch_block, masks[k - 1], count)
        parts.append(coefs[k] * lax.dot_general(left, moved_block, (((0,), (0,)), ((), ())), precision=HIGH, preferred_element_type=jnp.float32))
    return jnp.concatenate(parts, axis=1)

def newton_root(mat, eye):
    fro = jnp.sqrt(jnp.sum(mat * mat))
    approx = mat / (fro + 1e-06)
    inverse = eye
    for step in range(NS_ITERS):
        middle = 1.5 * eye - 0.5 * jnp.dot(inverse, approx, precision=HIGH)
        approx = jnp.dot(approx, middle, precision=HIGH)
        inverse = jnp.dot(middle, inverse, precision=HIGH)
    return (approx, inverse, fro)

def reference(factor, gates, gate_layout, jump_masks, jump_rates, sketch_perm, bases, basis_index):
    lows = ROWS_DEV // N_WIDE
    blocks = factor.reshape(N_WIDE, ROWS_DEV // GATE_ORD, GATE_ORD, RANK)
    layout = gate_layout.reshape(N_WIDE, ROWS_DEV // GATE_ORD)
    gated = lax.map(lambda pair: apply_blocks(gates, pair[1], pair[0]), (blocks, layout))
    moved = gated.reshape(N_WIDE, N_WIDE, lows, RANK).transpose(1, 0, 2, 3).reshape(N_WIDE, ROWS_DEV, RANK)
    keep = 1.0 - 0.5 * jnp.sum(jump_rates)
    coefs = [keep] + [jnp.sqrt(jump_rates[k]) for k in range(JUMPS)]
    table = sketch_table(sketch_perm, RANK)
    sketch = lax.map(lambda block: mixed_stack(block, table, coefs, jump_masks, N_WIDE), moved)
    partial_grams = lax.map(lambda block: lax.dot_general(block, block, (((0,), (0,)), ((), ())), precision=HIGH, preferred_element_type=jnp.float32), sketch)
    gram = lax.optimization_barrier(jnp.sum(partial_grams, axis=0))
    eye = jnp.eye(RANK, dtype=jnp.float32)
    unused, inverse, fro = newton_root(gram, eye)
    partial_proj = lax.map(lambda pair: project_block(pair[0], pair[1], coefs, jump_masks, N_WIDE), (sketch, moved))
    proj = lax.optimization_barrier(jnp.sum(partial_proj, axis=0))
    coeff = lax.dot_general(inverse, proj, (((0,), (0,)), ((), ())), precision=HIGH, preferred_element_type=jnp.float32)
    core = lax.dot_general(coeff, coeff, (((1,), (1,)), ((), ())), precision=HIGH, preferred_element_type=jnp.float32)
    approx_two, unused_two, fro_two = newton_root(core, eye)
    root = jnp.sqrt(fro_two + 1e-06) * approx_two
    mixing = jnp.dot(inverse, root, precision=HIGH)
    new_blocks = lax.map(lambda block: jnp.dot(block, mixing, precision=HIGH), sketch)
    rotated_in = new_blocks.reshape(N_WIDE, ROWS_DEV // ROT_ORD, ROT_ORD, RANK)

    def outcome(pair):
        rotated = apply_blocks(bases, pair[1], pair[0])
        return lax.optimization_barrier(jnp.sum(rotated * rotated, axis=2)).reshape(ROWS_DEV) / RANK
    weights = lax.map(outcome, (rotated_in, basis_index))
    return (new_blocks.reshape(ROWS, RANK), weights)
```

```python
import functools

import jax
import jax.numpy as jnp
from jax import lax
from jax.experimental import pallas as pl
from jax.experimental.pallas import tpu as pltpu
from jax.sharding import PartitionSpec as P

NS_ITERS = 7
MESH = pl.DeviceIdType.MESH
VMEM = pl.BlockSpec(memory_space=pltpu.VMEM)
SMEM = pl.BlockSpec(memory_space=pltpu.SMEM)
HBM = pl.BlockSpec(memory_space=pltpu.HBM)
LIMIT = 48 * 1024 * 1024
NN = (((1,), (0,)), ((), ()))
TN = (((0,), (0,)), ((), ()))
NT = (((1,), (1,)), ((), ()))


def split2(x):
    high = x.astype(jnp.bfloat16)
    return high, (x - high.astype(jnp.float32)).astype(jnp.bfloat16)


def split3(x):
    high = x.astype(jnp.bfloat16)
    rest = x - high.astype(jnp.float32)
    middle = rest.astype(jnp.bfloat16)
    return high, middle, (rest - middle.astype(jnp.float32)).astype(jnp.bfloat16)


def bdot(a, b, dims):
    return lax.dot_general(a, b, dims, preferred_element_type=jnp.float32)


def dot3(a, b, dims=NN):
    ah, al = a if isinstance(a, tuple) else split2(a)
    bh, bl = b if isinstance(b, tuple) else split2(b)
    return bdot(ah, bh, dims) + (bdot(ah, bl, dims) + bdot(al, bh, dims))


def remote(src, dst, send_sem, recv_sem, device):
    return pltpu.make_async_remote_copy(
        src_ref=src, dst_ref=dst, send_sem=send_sem, recv_sem=recv_sem, device_id=device, device_id_type=MESH
    )


def exchange_kernel(
    count, layout_ref, perm_ref, gates_ref, factor_ref, moved_ref, table_ref,
    held_gates, held, gated, layout, load_sem, send_sem, recv_sem, pass_sem, got_sem,
):
    me = lax.axis_index("wide")
    col = lax.axis_index("cols")
    partner = (me, 1 - col)
    rows, width = held.shape
    order = held_gates.shape[1]
    lows = rows // count
    blocks = rows // order
    load_gates = pltpu.make_async_copy(gates_ref, held_gates, load_sem.at[0])
    load_factor = pltpu.make_async_copy(factor_ref, held, load_sem.at[1])
    load_layout = pltpu.make_async_copy(layout_ref, layout, load_sem.at[2])
    load_layout.start()
    load_gates.start()
    load_factor.start()
    barrier = pltpu.get_barrier_semaphore()

    def signal(d, carry):
        pl.semaphore_signal(barrier, inc=1, device_id=(lax.rem(me + d, count), col), device_id_type=MESH)
        return carry

    lax.fori_loop(1, count, signal, 0)
    pl.semaphore_signal(barrier, inc=1, device_id=partner, device_id_type=MESH)

    def outgoing(h):
        at = pl.ds(pl.multiple_of(h * lows, lows), lows)
        return remote(gated.at[at, :], moved_ref.at[col, me], send_sem.at[h], recv_sem.at[me], (h, col))

    def forward(s):
        return remote(moved_ref.at[col, s], moved_ref.at[col, s], pass_sem.at[s], got_sem.at[s], partner)

    per = order // lows
    unroll = 4 if blocks % 4 == 0 else 1
    first = me // per + 1

    def gate(i):
        for u in range(unroll):
            b = lax.rem(first + i * unroll + u, blocks)
            at = pl.ds(pl.multiple_of(b * order, order), order)
            gated[at, :] = dot3(held_gates[layout[b]], held[at, :])

    def send(i):
        for u in range(unroll):
            b = lax.rem(first + i * unroll + u, blocks)
            for j in range(per):
                h = b * per + j

                @pl.when(h != me)
                def _():
                    outgoing(h).start()

    load_layout.wait()
    load_gates.wait()
    load_factor.wait()
    gate(0)
    pl.semaphore_wait(barrier, count)

    def step(i, carry):
        gate(i)
        send(i - 1)
        return carry

    lax.fori_loop(1, blocks // unroll, step, 0)
    send(blocks // unroll - 1)
    own = pl.ds(pl.multiple_of(me * lows, lows), lows)
    moved_ref[col, me] = gated[own, :]
    remote(gated.at[own, :], moved_ref.at[col, me], pass_sem.at[me], got_sem.at[me], partner).start()

    rank, stacked = table_ref.shape
    perm = perm_ref[...]
    strip = 64
    for r in range(0, rank, strip):
        target = lax.broadcasted_iota(jnp.int32, (strip, stacked), 0) + r
        piece = jnp.zeros((strip, stacked), jnp.float32)
        for k in range(stacked // rank):
            piece = jnp.where(perm == target + k * rank, 1.0 - 2.0 * (k % 2), piece)
        table_ref[r:r + strip, :] = piece.astype(jnp.bfloat16)

    def relay(i, carry):
        s = lax.rem(me + count - i, count)
        arrived = moved_ref.at[col, s]
        remote(arrived, arrived, send_sem.at[s], recv_sem.at[s], (s, col)).wait_recv()
        forward(s).start()
        return carry

    lax.fori_loop(1, count, relay, 0)

    def drain(d, carry):
        outgoing(lax.rem(me + d, count)).wait_send()
        return carry

    lax.fori_loop(1, count, drain, 0)

    def finish(d, carry):
        s = lax.rem(me + count - d, count)
        forward(s).wait_send()
        remote(moved_ref.at[1 - col, s], moved_ref.at[1 - col, s], pass_sem.at[s], got_sem.at[s], partner).wait_recv()
        return carry

    lax.fori_loop(0, count, finish, 0)


def sketch_kernel(
    groups, mask_ref, rate_ref, moved_ref, table_ref, sketch_ref, full_ref,
    high, low, part, inbox, sums, lanes, masks, rates_held, load_sem,
    near_send, near_recv, far_send, far_recv, out_send, out_recv, spread_send, spread_recv, pass_sem, got_sem,
):
    me = lax.axis_index("wide")
    col = lax.axis_index("cols")
    partner = (me, 1 - col)
    near, far = part.shape[:2]
    p = lax.rem(me, near)
    o = me // near

    def beside(i):
        return lax.rem(p + i, near)

    def beyond(i):
        return lax.rem(o + i, far)

    def device(there, q):
        return (there * near + q, col)

    load_masks = pltpu.make_async_copy(mask_ref, masks, load_sem.at[0])
    load_rates = pltpu.make_async_copy(rate_ref, rates_held, load_sem.at[1])
    load_masks.start()
    load_rates.start()
    barrier = pltpu.get_barrier_semaphore()
    for i in range(1, near):
        pl.semaphore_signal(barrier, inc=1, device_id=device(o, beside(i)), device_id_type=MESH)
    for i in range(1, far):
        pl.semaphore_signal(barrier, inc=1, device_id=device(beyond(i), p), device_id_type=MESH)
    pl.semaphore_signal(barrier, inc=1, device_id=partner, device_id_type=MESH)

    halves, count, lows, width = moved_ref.shape
    rows, stacked = high.shape
    rank = halves * width
    terms = stacked // rank
    load_masks.wait()
    load_rates.wait()
    rates = [rates_held[k] for k in range(terms - 1)]
    coefs = [jnp.full((1, width), 1.0 - 0.5 * sum(rates), jnp.float32)]
    coefs += [jnp.sqrt(jnp.full((1, width), rate, jnp.float32)) for rate in rates]

    def fill(w, carry):
        at = pl.ds(pl.multiple_of(w * lows, lows), lows)
        for k in range(terms):
            source = w if k == 0 else jnp.bitwise_xor(w, masks[k - 1])
            for half in range(halves):
                top, rest = split2(coefs[k] * moved_ref[half, source])
                columns = slice(k * rank + half * width, k * rank + (half + 1) * width)
                high[at, columns] = top
                low[at, columns] = rest
        return carry

    lax.fori_loop(0, count, fill, 0)
    tile = min(rows, 512)
    for t in range(rows // tile):
        at = slice(t * tile, (t + 1) * tile)
        sketch_ref[at, :] = bdot(high[at, :], table_ref[...], NT) + bdot(low[at, :], table_ref[...], NT)
    mine = split2(sketch_ref[:, pl.ds(pl.multiple_of(col * width, width), width)])
    deep, wide = part.shape[2:]
    step = min(wide, rank)
    for k in range(terms):
        columns = slice(k * rank, (k + 1) * rank)
        value = dot3(mine, (high[:, columns], low[:, columns]), TN)
        pieces = []
        for g in range(k * rank // wide, max(k * rank // wide + 1, (k + 1) * rank // wide)):
            start = max(0, k * rank - g * wide)
            for r in range(width // deep):
                q, there = divmod(r * groups + g, far)
                left = g * wide + start - k * rank
                part[q, there, :, start:start + step] = value[r * deep:(r + 1) * deep, left:left + step]
            pieces.append((g, start))
        if k == 0:
            pl.semaphore_wait(barrier, near + far - 1)
        for g, start in pieces:
            for r in range(width // deep):
                q, there = divmod(r * groups + g, far)

                @pl.when(q != p)
                def _():
                    remote(
                        part.at[q, there, :, start:start + step], inbox.at[p, there, :, start:start + step],
                        near_send.at[q, there], near_recv.at[p, there], device(o, q),
                    ).start()

    def near_copy(q, there):
        return remote(part.at[q, there], inbox.at[p, there], near_send.at[q, there], near_recv.at[p, there], device(o, q))

    def far_copy(there):
        return remote(sums.at[there], lanes.at[o], far_send.at[there], far_recv.at[o], device(there, p))

    for j in range(1, far + 1):
        there = beyond(j)
        value = part[p, there]
        for i in range(1, near):
            q = beside(i)
            remote(
                inbox.at[q, there], inbox.at[q, there], near_send.at[q, there], near_recv.at[q, there], device(o, q)
            ).wait_recv()
            value = value + inbox[q, there]
        sums[there] = value
        if j < far:
            far_copy(there).start()
    value = sums[o]
    for j in range(1, far):
        there = beyond(j)
        remote(lanes.at[there], lanes.at[there], far_send.at[there], far_recv.at[there], device(there, p)).wait_recv()
        value = value + lanes[there]
    full_ref[col, p, o] = value
    for j in range(1, far + 1):
        for i in range(1, near):
            near_copy(beside(i), beyond(j)).wait_send()
    for j in range(1, far):
        far_copy(beyond(j)).wait_send()

    def out_copy(there):
        return remote(full_ref.at[col, p, o], full_ref.at[col, p, o], out_send.at[there], out_recv.at[o], device(there, p))

    def spread_copy(q, there):
        block = full_ref.at[col, p, there]
        return remote(block, block, spread_send.at[q, there], spread_recv.at[p, there], device(o, q))

    def pass_copy(q, there):
        block = full_ref.at[col, q, there]
        return remote(block, block, pass_sem.at[q, there], got_sem.at[q, there], partner)

    def spread(there):
        for i in range(1, near):
            spread_copy(beside(i), there).start()
        pass_copy(p, there).start()

    for j in range(1, far):
        out_copy(beyond(j)).start()
    spread(o)
    for j in range(1, far):
        there = lax.rem(o + far - j, far)
        block = full_ref.at[col, p, there]
        remote(block, block, out_send.at[there], out_recv.at[there], device(there, p)).wait_recv()
        spread(there)
    for j in range(far):
        there = lax.rem(o + far - j, far)
        for i in range(1, near):
            q = lax.rem(p + near - i, near)
            block = full_ref.at[col, q, there]
            remote(block, block, spread_send.at[q, there], spread_recv.at[q, there], device(o, q)).wait_recv()
            pass_copy(q, there).start()
    for j in range(1, far):
        out_copy(beyond(j)).wait_send()
    for j in range(far):
        there = lax.rem(o + far - j, far)
        for i in range(1, near):
            spread_copy(beside(i), there).wait_send()
        for i in range(near):
            q = lax.rem(p + near - i, near)
            pass_copy(q, there).wait_send()
            block = full_ref.at[1 - col, q, there]
            remote(block, block, pass_sem.at[q, there], got_sem.at[q, there], partner).wait_recv()


def newton_root(mat, eye, need_inverse):
    fro = jnp.sqrt(jnp.sum(mat * mat))
    approx = mat / (fro + 1e-06)
    middle = 1.5 * eye - 0.5 * approx
    approx = dot3(approx, middle)
    inverse = middle
    for step in range(1, NS_ITERS):
        inv2 = split2(inverse)
        app2 = split2(approx)
        mid2 = split2(1.5 * eye - 0.5 * dot3(inv2, app2))
        last = step == NS_ITERS - 1
        if not (last and need_inverse):
            approx = dot3(app2, mid2)
        if not last or need_inverse:
            inverse = dot3(mid2, inv2)
    return (inverse if need_inverse else approx), fro


def finish_kernel(index_ref, proj_ref, table_ref, sketch_ref, bases_ref, new_ref, weight_ref, fresh, squares, store_sem):
    col = lax.axis_index("cols")
    rank = proj_ref.shape[0]
    rows = sketch_ref.shape[0]
    width = new_ref.shape[1]
    rot = bases_ref.shape[1]
    row = lax.broadcasted_iota(jnp.int32, (rank, rank), 0)
    column = lax.broadcasted_iota(jnp.int32, (rank, rank), 1)
    eye = jnp.where(row == column, 1.0, 0.0).astype(jnp.float32)
    proj = proj_ref[...]
    ph, pm, plow = split3(proj)
    table = table_ref[...]
    gram = bdot(ph, table, NT) + (bdot(pm, table, NT) + bdot(plow, table, NT))
    inverse, _ = newton_root(gram, eye, True)
    inv2 = split2(inverse)
    coeff = split2(dot3(inv2, (ph, pm), TN))
    core = dot3(coeff, coeff, NT)
    approx, fro = newton_root(core, eye, False)
    mixing = split2(dot3(inv2, split2(jnp.sqrt(fro + 1e-06) * approx)))
    tile = min(rows, 512)
    mine = pl.ds(pl.multiple_of(col * width, width), width)
    stores = []
    for t in range(rows // tile):
        at = slice(t * tile, (t + 1) * tile)
        fresh[at, :] = dot3(sketch_ref[at, :], mixing)
        store = pltpu.make_async_copy(fresh.at[at, mine], new_ref.at[at, :], store_sem.at[t])
        store.start()
        stores.append(store)
    share = squares.shape[0]
    for i in range(share // rot):
        start = pl.multiple_of(col * share + i * rot, rot)
        turned = dot3(bases_ref[index_ref[col * (share // rot) + i]], fresh[pl.ds(start, rot), :])
        squares[i * rot:(i + 1) * rot, :] = turned * turned
    ones = jnp.ones((8, rank), jnp.bfloat16)
    sh, sm, sl = split3(squares[...])
    sums = bdot(ones, sh, NT) + (bdot(ones, sm, NT) + bdot(ones, sl, NT))
    weight_ref[...] = sums[0:1, :] / rank
    for store in stores:
        store.wait()


def per_device(factor, gates, gate_layout, jump_masks, jump_rates, sketch_perm, bases, basis_index):
    rows, width = factor.shape
    count = lax.axis_size("wide")
    halves = lax.axis_size("cols")
    rank = width * halves
    stacked = sketch_perm.shape[0]
    lows = rows // count
    f32 = jnp.float32
    bf16 = jnp.bfloat16

    def dma(*shape):
        return pltpu.SemaphoreType.DMA(shape)

    def stay(x):
        return pltpu.with_memory_space_constraint(x, pltpu.HBM)

    factor, gates, gate_layout, jump_masks, jump_rates = map(stay, (factor, gates, gate_layout, jump_masks, jump_rates))

    moved, table = pl.pallas_call(
        functools.partial(exchange_kernel, count),
        out_shape=[
            jax.ShapeDtypeStruct((halves, count, lows, width), f32),
            jax.ShapeDtypeStruct((rank, stacked), bf16),
        ],
        in_specs=[HBM, VMEM, HBM, HBM],
        out_specs=[VMEM, VMEM],
        scratch_shapes=[
            pltpu.VMEM(gates.shape, f32),
            pltpu.VMEM((rows, width), f32),
            pltpu.VMEM((rows, width), f32),
            pltpu.SMEM(gate_layout.shape, jnp.int32),
            dma(3), dma(count), dma(count), dma(count), dma(count),
        ],
        compiler_params=pltpu.CompilerParams(collective_id=0, has_side_effects=True, vmem_limit_bytes=LIMIT),
        name="exchange",
    )(gate_layout, sketch_perm.reshape(1, stacked), gates, factor)

    deep = max(8, width // count)
    groups = count * deep // width
    wide = stacked // groups
    near = 1
    while near * near * 4 <= count:
        near *= 2
    far = count // near
    sketch, full = pl.pallas_call(
        functools.partial(sketch_kernel, groups),
        out_shape=[
            jax.ShapeDtypeStruct((rows, rank), f32),
            jax.ShapeDtypeStruct((halves, near, far, deep, wide), f32),
        ],
        in_specs=[HBM, HBM, VMEM, VMEM],
        out_specs=[VMEM, VMEM],
        scratch_shapes=[
            pltpu.VMEM((rows, stacked), bf16),
            pltpu.VMEM((rows, stacked), bf16),
            pltpu.VMEM((near, far, deep, wide), f32),
            pltpu.VMEM((near, far, deep, wide), f32),
            pltpu.VMEM((far, deep, wide), f32),
            pltpu.VMEM((far, deep, wide), f32),
            pltpu.SMEM(jump_masks.shape, jnp.int32),
            pltpu.SMEM(jump_rates.shape, f32),
            dma(2), dma(near, far), dma(near, far), dma(far), dma(far), dma(far), dma(far),
            dma(near, far), dma(near, far), dma(near, far), dma(near, far),
        ],
        compiler_params=pltpu.CompilerParams(collective_id=1, has_side_effects=True, vmem_limit_bytes=LIMIT),
        name="sketch",
    )(jump_masks, jump_rates, moved, table)
    proj = full.reshape(halves, count // groups, groups, deep, wide).transpose(0, 1, 3, 2, 4).reshape(rank, stacked)

    return pl.pallas_call(
        finish_kernel,
        out_shape=[
            jax.ShapeDtypeStruct((rows, width), f32),
            jax.ShapeDtypeStruct((1, rows // halves), f32),
        ],
        in_specs=[SMEM, VMEM, VMEM, VMEM, VMEM],
        out_specs=[HBM, VMEM],
        scratch_shapes=[
            pltpu.VMEM((rows, rank), f32),
            pltpu.VMEM((rows // halves, rank), f32),
            dma(max(1, rows // 512)),
        ],
        compiler_params=pltpu.CompilerParams(vmem_limit_bytes=LIMIT),
        name="finish",
    )(basis_index.reshape(-1), proj, table, sketch, bases)


def solution(mesh):
    return jax.shard_map(
        per_device,
        mesh=mesh,
        in_specs=(P("wide", "cols"), P(), P("wide"), P(), P(), P(), P(), P("wide", None)),
        out_specs=(P("wide", "cols"), P("wide", "cols")),
        check_vma=False,
    )
```
